128 devices in a mesh: ctx: 8 (over z, core), kv: 8 (over x_hi, y), grp: 2 (over x_lo).
Axes of the slice: x: 4 (x_hi: 2, x_lo: 2; x = x_hi * 2 + x_lo), y: 4, z: 4, core: 2. Of those that a mesh axis runs over, the one named last changes fastest.
Arguments:
- queries: bfloat16 [2048, 4096], P('ctx', ('kv', 'grp')), may hold values from -6 to 6
- keys: bfloat16 [2048, 1024], P('ctx', 'kv'), may hold values from -6 to 6
- values: bfloat16 [2048, 1024], P('ctx', 'kv'), may hold values from -6 to 6
- out_grad: bfloat16 [2048, 4096], P('ctx', ('kv', 'grp')), may hold values from -0.15625 to 0.15625
Outputs:
- query_grad: bfloat16 [2048, 4096], P('ctx', ('kv', 'grp'))
- key_grad: bfloat16 [2048, 1024], P(('ctx', 'grp'), 'kv')
- value_grad: bfloat16 [2048, 1024], P(('ctx', 'grp'), 'kv')
The draws below stay inside these ranges and needn't reach their ends.
All inputs are finite; a program needn't handle non-finite values.
Results may differ from the reference program's by a relative error of at most 0.015.
Values may be sent and summed in bfloat16 or wider, within the bound.
A program may use at most 128 MiB of HBM per device.

```python
import jax
import jax.numpy as jnp
import numpy as np
from jax import lax

HEAD = 128
GROUP = 4
BLOCK = 256
KVH = 8
QH = 32
FEAT = 8256
TOKENS = 2048


def level_of(stream_key, shape, cuts, smallest, top_value):
    loudness = 1.0
    for axis_at, shards_of in cuts:
        draws = jax.random.uniform(jax.random.fold_in(jax.random.fold_in(stream_key, 6), axis_at), (shards_of,), jnp.float32, smallest / len(cuts), top_value / len(cuts))
        loudness = loudness * jnp.repeat(jnp.exp(draws), shape[axis_at] // shards_of).reshape((-1,) + (1,) * (len(shape) - 1 - axis_at))
    return loudness


def noise(key, extent, width, limit, cuts=(), held_as=jnp.bfloat16):
    array = jax.random.normal(key, extent, jnp.float32) * width
    if len(cuts) > 0:
        array = level_of(key, extent, cuts, -0.22, 0.18) * array
    return jnp.clip(array, min=-limit, max=limit).astype(held_as)


def setup_inputs(seed: int = 0) -> dict:
    arg_keys = jax.random.split(jax.random.key(seed), 5)
    queries = noise(arg_keys[0], (TOKENS, QH * HEAD), 1.0, 6.0, ((0, 8), (1, 16)))
    keys = noise(arg_keys[1], (TOKENS, KVH * HEAD), 1.0, 6.0, ((0, 8), (1, 8)))
    values = noise(arg_keys[2], (TOKENS, KVH * HEAD), 1.0, 6.0, ((0, 8), (1, 8)))
    out_grad = noise(arg_keys[3], (TOKENS, QH * HEAD), 0.01, 0.15625, ((0, 8), (1, 16)))
    return dict(queries=queries, keys=keys, values=values, out_grad=out_grad)


def tables(breadth):
    first_axis, second_axis = np.triu_indices(breadth)
    weights = np.where(first_axis == second_axis, 1.0, np.sqrt(2.0)) / np.sqrt(breadth)
    pair_map = np.zeros((breadth, breadth), np.int32)
    pair_map[first_axis, second_axis] = np.arange(first_axis.size)
    pair_map[second_axis, first_axis] = np.arange(first_axis.size)
    slopes = np.where(np.eye(breadth) > 0, 2.0, np.sqrt(2.0)) / np.sqrt(breadth)
    return (first_axis, second_axis, weights, pair_map.reshape(-1), slopes)

def expand(points_t, first_axis, second_axis, weights):
    values_t = points_t.astype(jnp.float32)
    scaling = jnp.asarray(weights, jnp.float32)[:, None]
    return (values_t[first_axis] * values_t[second_axis] * scaling).astype(jnp.bfloat16)

def unpack(state_low, pair_map):
    return state_low[pair_map]

def lift(state_full, cotangent_t, points_t, slopes):
    breadth = points_t.shape[0]
    unpacked = jnp.dot(state_full, cotangent_t, preferred_element_type=jnp.float32)
    unpacked = unpacked * jnp.asarray(slopes, jnp.float32).reshape(-1, 1)
    unpacked = unpacked.reshape(breadth, breadth, cotangent_t.shape[1])
    return lax.optimization_barrier(jnp.sum(unpacked * points_t.astype(jnp.float32)[None, :, :], axis=1))

def within_block(query_rows, key_rows, value_rows, grad_rows, breadth):
    length = key_rows.shape[0]
    causal = jnp.arange(length)[:, None] >= jnp.arange(length)[None, :]
    scores = jnp.dot(query_rows, key_rows.T, preferred_element_type=jnp.float32)
    weight_low = jnp.where(causal, scores * scores / breadth, 0.0).astype(jnp.bfloat16)
    mixing = jnp.dot(grad_rows, value_rows.T, preferred_element_type=jnp.float32)
    slope_low = jnp.where(causal, 2.0 * scores * mixing / breadth, 0.0).astype(jnp.bfloat16)
    query_part = jnp.dot(slope_low, key_rows, preferred_element_type=jnp.float32)
    key_part = jnp.dot(slope_low.T, query_rows, preferred_element_type=jnp.float32)
    value_part = jnp.dot(weight_low.T, grad_rows, preferred_element_type=jnp.float32)
    return (query_part, key_part, value_part)

def reference(queries, keys, values, out_grad):
    first_axis, second_axis, weights, pair_map, slopes = tables(HEAD)
    blocks = TOKENS // BLOCK
    key_heads = keys.reshape(blocks, BLOCK, KVH, HEAD).transpose(2, 0, 1, 3)
    value_heads = values.reshape(blocks, BLOCK, KVH, HEAD).transpose(2, 0, 1, 3)
    query_heads = queries.reshape(blocks, BLOCK, KVH, GROUP, HEAD).transpose(2, 0, 3, 1, 4)
    grad_heads = out_grad.reshape(blocks, BLOCK, KVH, GROUP, HEAD).transpose(2, 0, 3, 1, 4)

    def one_head(operands):
        key_blocks, value_blocks, query_blocks, grad_blocks = operands
        zeros = jnp.zeros((FEAT, HEAD), jnp.float32)

        def forward(carry, pieces):
            key_rows, value_rows = pieces
            expanded = expand(key_rows.T, first_axis, second_axis, weights)
            return (carry + jnp.dot(expanded, value_rows, preferred_element_type=jnp.float32), carry.astype(jnp.bfloat16))
        unused, prefix = lax.scan(forward, zeros, (key_blocks, value_blocks))

        def backward(carry, pieces):
            query_rows, grad_rows = pieces
            summed = carry
            for member in range(GROUP):
                expanded = expand(query_rows[member].T, first_axis, second_axis, weights)
                summed = summed + jnp.dot(expanded, grad_rows[member], preferred_element_type=jnp.float32)
            return (summed, carry.astype(jnp.bfloat16))
        unused, suffix = lax.scan(backward, zeros, (query_blocks, grad_blocks), reverse=True)

        def one_block(pieces):
            key_rows, value_rows, query_rows, grad_rows, before, after = pieces
            before_full = unpack(before, pair_map)
            after_full = unpack(after, pair_map)
            key_sum = jnp.zeros((BLOCK, HEAD), jnp.float32)
            value_sum = jnp.zeros((BLOCK, HEAD), jnp.float32)
            query_out = []
            for member in range(GROUP):
                query_part, key_part, value_part = within_block(query_rows[member], key_rows, value_rows, grad_rows[member], HEAD)
                query_part = query_part + lift(before_full, grad_rows[member].T, query_rows[member].T, slopes).T
                query_out.append(query_part.astype(jnp.bfloat16))
                key_sum = key_sum + key_part
                value_sum = value_sum + value_part
            key_sum = key_sum + lift(after_full, value_rows.T, key_rows.T, slopes).T
            expanded = expand(key_rows.T, first_axis, second_axis, weights)
            value_sum = value_sum + jnp.dot(expanded.T, after, preferred_element_type=jnp.float32)
            return (jnp.stack(query_out), key_sum.astype(jnp.bfloat16), value_sum.astype(jnp.bfloat16))
        return lax.map(one_block, (key_blocks, value_blocks, query_blocks, grad_blocks, prefix, suffix))
    query_grad, key_grad, value_grad = lax.map(one_head, (key_heads, value_heads, query_heads, grad_heads))
    query_grad = query_grad.transpose(1, 3, 0, 2, 4).reshape(TOKENS, QH * HEAD)
    key_grad = key_grad.transpose(1, 2, 0, 3).reshape(TOKENS, KVH * HEAD)
    value_grad = value_grad.transpose(1, 2, 0, 3).reshape(TOKENS, KVH * HEAD)
    return (query_grad, key_grad, value_grad)
```

```python
import jax
import jax.numpy as jnp
from jax import lax
from jax.experimental import pallas as pl
from jax.experimental.pallas import tpu as pltpu
from jax.sharding import PartitionSpec as P

BLOCK = 256
HEAD = 128
HALF = 128
CHIPS = 4
MESH = pl.DeviceIdType.MESH
F32 = jnp.float32
BF16 = jnp.bfloat16


def dot(a, b, contract):
    return lax.dot_general(a, b, ((contract[:1], contract[1:]), ((), ())), preferred_element_type=F32)


def tile(key_rows, value_rows, query_rows, grad_rows, masked):
    scores = dot(key_rows, query_rows, (1, 1))
    mixing = dot(value_rows, grad_rows, (1, 1))
    if masked:
        at = lax.broadcasted_iota(jnp.int32, scores.shape, 0)
        seen_by = lax.broadcasted_iota(jnp.int32, scores.shape, 1)
        scores = jnp.where(at <= seen_by, scores, 0.0)
    weight_low = (scores * scores).astype(BF16)
    slope_low = (scores * mixing).astype(BF16)
    value_part = dot(weight_low, grad_rows, (1, 0))
    key_part = dot(slope_low, query_rows, (1, 0))
    query_part = dot(slope_low, key_rows, (0, 0))
    return query_part, key_part, value_part


def kernel(
    q_hbm, k_hbm, v_hbm, g_hbm,
    query_out, key_out, value_out,
    q, k, v, g, other_q, other_g, far_k, far_v,
    query_sum, key_sum, value_sum, other_send, other_recv, side_send, side_recv, far_send, far_recv,
    load_sem, other_send_sem, other_recv_sem, far_kv_send_sem, far_kv_recv_sem,
    far_send_sem, far_recv_sem, side_send_sem, side_recv_sem, back_send_sem, back_recv_sem,
):
    ctx = lax.axis_index("ctx")
    chip, core = ctx // 2, lax.rem(ctx, 2)
    grp = lax.axis_index("grp")

    def at(chip_to, core_to, grp_to):
        return {"ctx": chip_to * 2 + core_to, "grp": grp_to}

    twin = at(chip, 1 - core, grp)
    side = at(chip, core, 1 - grp)

    loads = [
        pltpu.make_async_copy(src, dst, load_sem.at[i])
        for i, (src, dst) in enumerate(((k_hbm, k), (q_hbm, q), (v_hbm, v), (g_hbm, g)))
    ]
    for copy in loads:
        copy.start()

    barrier = pltpu.get_barrier_semaphore()
    pl.semaphore_signal(barrier, inc=1, device_id=twin, device_id_type=MESH)
    pl.semaphore_signal(barrier, inc=1, device_id=side, device_id_type=MESH)
    for step in range(1, CHIPS):
        to = lax.rem(chip + step, CHIPS)
        for grp_to in (grp, 1 - grp):
            pl.semaphore_signal(barrier, inc=1, device_id=at(to, core, grp_to), device_id_type=MESH)
    pl.semaphore_wait(barrier, 2 + 2 * (CHIPS - 1))

    def remote(src, dst, send, recv, to):
        return pltpu.make_async_remote_copy(
            src_ref=src, dst_ref=dst, send_sem=send, recv_sem=recv, device_id=to, device_id_type=MESH
        )

    def kv_copies(step):
        to = at(lax.rem(chip + step, CHIPS), core, grp)
        slot = step - 1
        return (
            remote(k_hbm, far_k.at[slot], far_kv_send_sem.at[slot, 0], far_kv_recv_sem.at[slot, 0], to),
            remote(v_hbm, far_v.at[slot], far_kv_send_sem.at[slot, 1], far_kv_recv_sem.at[slot, 1], to),
        )

    def far_copies(step):
        slot = step - 1
        return [
            remote(
                far_send.at[slot, half], far_recv.at[slot, grp], far_send_sem.at[slot, half],
                far_recv_sem.at[slot, grp], at(lax.rem(chip - step + CHIPS, CHIPS), core, half),
            )
            for half in range(2)
        ]

    for step in (1, 3, 2):
        @pl.when(chip + step < CHIPS)
        def _():
            for copy in kv_copies(step):
                copy.start()

    other_copies = (
        remote(q_hbm, other_q, other_send_sem.at[0], other_recv_sem.at[0], twin),
        remote(g_hbm, other_g, other_send_sem.at[1], other_recv_sem.at[1], twin),
    )
    for copy in other_copies:
        copy.start()
    for copy in loads:
        copy.wait()

    def columns(head):
        return slice(head * HEAD, (head + 1) * HEAD)

    key_total = jnp.zeros((BLOCK, HEAD), F32)
    value_total = jnp.zeros((BLOCK, HEAD), F32)
    for head in range(2):
        query_part, key_part, value_part = tile(
            k[...], v[...], q[:, columns(head)], g[:, columns(head)], True
        )
        query_sum[0, head] = query_part
        query_sum[1, head] = jnp.zeros_like(query_part)
        key_total += key_part
        value_total += value_part
    key_sum[...] = key_total
    value_sum[...] = value_total
    for copy in other_copies:
        copy.wait()

    @pl.when(core == 0)
    def _():
        key_more = jnp.zeros((BLOCK, HEAD), F32)
        value_more = jnp.zeros((BLOCK, HEAD), F32)
        for head in range(2):
            query_part, key_part, value_part = tile(
                k[...], v[...], other_q[:, columns(head)], other_g[:, columns(head)], False
            )
            query_sum[1, head] += query_part
            key_more += key_part
            value_more += value_part
        key_sum[...] += key_more
        value_sum[...] += value_more

    away = pl.ds(pl.multiple_of((1 - grp) * HALF, HALF), HALF)
    mine = pl.ds(pl.multiple_of(grp * HALF, HALF), HALF)
    side_send[:, columns(0)] = (key_sum[away] * (2.0 / HEAD)).astype(BF16)
    side_send[:, columns(1)] = (value_sum[away] * (1.0 / HEAD)).astype(BF16)
    side_copy = remote(side_send, side_recv, side_send_sem, side_recv_sem, side)
    side_copy.start()

    for step in range(1, CHIPS):
        slot = step - 1

        @pl.when(chip >= step)
        def _():
            for copy in kv_copies(step):
                copy.wait_recv()
            far_key = jnp.zeros((BLOCK, HEAD), F32)
            far_value = jnp.zeros((BLOCK, HEAD), F32)
            for part, (rows, grads) in enumerate(((q, g), (other_q, other_g))):
                for head in range(2):
                    query_part, key_part, value_part = tile(
                        far_k[slot], far_v[slot], rows[:, columns(head)], grads[:, columns(head)], False
                    )
                    query_sum[part, head] += query_part
                    far_key += key_part
                    far_value += value_part
            far_key = (far_key * (2.0 / HEAD)).astype(BF16)
            far_value = (far_value * (1.0 / HEAD)).astype(BF16)
            for half in range(2):
                far_send[slot, half, :, columns(0)] = far_key[half * HALF:(half + 1) * HALF]
                far_send[slot, half, :, columns(1)] = far_value[half * HALF:(half + 1) * HALF]
            for copy in far_copies(step):
                copy.start()

    for head in range(2):
        other_send[:, columns(head)] = query_sum[1, head]
    back = remote(other_send, other_recv, back_send_sem, back_recv_sem, twin)
    back.start()

    for step in range(1, CHIPS):
        @pl.when(chip + step < CHIPS)
        def _():
            for copy in kv_copies(step):
                copy.wait_send()

    back.wait()
    for head in range(2):
        query_out[:, columns(head)] = (
            (query_sum[0, head] + other_recv[:, columns(head)]) * (2.0 / HEAD)
        ).astype(BF16)

    side_copy.wait()
    key_sum[:HALF] = key_sum[mine] * (2.0 / HEAD) + side_recv[:, columns(0)].astype(F32)
    value_sum[:HALF] = value_sum[mine] * (1.0 / HEAD) + side_recv[:, columns(1)].astype(F32)

    for step in range(1, CHIPS):
        slot = step - 1

        @pl.when(chip + step < CHIPS)
        def _():
            for grp_from in range(2):
                remote(
                    far_send.at[slot, 0], far_recv.at[slot, grp_from], far_send_sem.at[slot, 0],
                    far_recv_sem.at[slot, grp_from], side,
                ).wait_recv()
                key_sum[:HALF] += far_recv[slot, grp_from, :, columns(0)].astype(F32)
                value_sum[:HALF] += far_recv[slot, grp_from, :, columns(1)].astype(F32)

    for step in range(1, CHIPS):
        @pl.when(chip >= step)
        def _():
            for copy in far_copies(step):
                copy.wait_send()
    key_out[...] = key_sum[:HALF].astype(BF16)
    value_out[...] = value_sum[:HALF].astype(BF16)


def local(queries, keys, values, out_grad):
    steps = CHIPS - 1
    dma = pltpu.SemaphoreType.DMA
    return pl.pallas_call(
        kernel,
        out_shape=(
            jax.ShapeDtypeStruct((BLOCK, 2 * HEAD), BF16),
            jax.ShapeDtypeStruct((HALF, HEAD), BF16),
            jax.ShapeDtypeStruct((HALF, HEAD), BF16),
        ),
        in_specs=[pl.BlockSpec(memory_space=pl.ANY)] * 4,
        out_specs=(pl.BlockSpec(memory_space=pltpu.VMEM),) * 3,
        scratch_shapes=[
            pltpu.VMEM((BLOCK, 2 * HEAD), BF16),
            pltpu.VMEM((BLOCK, HEAD), BF16),
            pltpu.VMEM((BLOCK, HEAD), BF16),
            pltpu.VMEM((BLOCK, 2 * HEAD), BF16),
            pltpu.VMEM((BLOCK, 2 * HEAD), BF16),
            pltpu.VMEM((BLOCK, 2 * HEAD), BF16),
            pltpu.VMEM((steps, BLOCK, HEAD), BF16),
            pltpu.VMEM((steps, BLOCK, HEAD), BF16),
            pltpu.VMEM((2, 2, BLOCK, HEAD), F32),
            pltpu.VMEM((BLOCK, HEAD), F32),
            pltpu.VMEM((BLOCK, HEAD), F32),
            pltpu.VMEM((BLOCK, 2 * HEAD), F32),
            pltpu.VMEM((BLOCK, 2 * HEAD), F32),
            pltpu.VMEM((HALF, 2 * HEAD), BF16),
            pltpu.VMEM((HALF, 2 * HEAD), BF16),
            pltpu.VMEM((steps, 2, HALF, 2 * HEAD), BF16),
            pltpu.VMEM((steps, 2, HALF, 2 * HEAD), BF16),
            dma((4,)), dma((2,)), dma((2,)), dma((steps, 2)), dma((steps, 2)),
            dma((steps, 2)), dma((steps, 2)), dma, dma, dma, dma,
        ],
        compiler_params=pltpu.CompilerParams(collective_id=0, has_side_effects=True),
    )(queries, keys, values, out_grad)


def solution(mesh):
    return jax.shard_map(
        local,
        mesh=mesh,
        in_specs=(P("ctx", ("kv", "grp")), P("ctx", "kv"), P("ctx", "kv"), P("ctx", ("kv", "grp"))),
        out_specs=(P("ctx", ("kv", "grp")), P(("ctx", "grp"), "kv"), P(("ctx", "grp"), "kv")),
        check_vma=False,
    )
```

```python
import jax
import jax.numpy as jnp
from jax import lax
from jax.experimental import pallas as pl
from jax.experimental.pallas import tpu as pltpu
from jax.sharding import PartitionSpec as P

BLOCK = 256
HEAD = 128
HALF = 128
CHIPS = 4
STEPS = CHIPS - 1
MESH = pl.DeviceIdType.MESH
F32 = jnp.float32
BF16 = jnp.bfloat16
SLOPE = 2.0 / HEAD
WEIGHT = 1.0 / HEAD


def dot(a, b, contract):
    return lax.dot_general(a, b, ((contract[:1], contract[1:]), ((), ())), preferred_element_type=F32)


def columns(head):
    return slice(head * HEAD, (head + 1) * HEAD)


def kernel(
    q_hbm, k_hbm, v_hbm, g_hbm,
    query_out, key_out, value_out,
    q, g, kv, far_kv, weights, slopes, far_slopes,
    query_sum, key_sum, value_sum, back_recv, side_send, side_recv, far_send, far_recv,
    load_sem, other_send_sem, other_recv_sem, kv_send_sem, pass_send_sem, kv_recv_sem,
    far_send_sem, far_recv_sem, side_send_sem, side_recv_sem, back_send_sem, back_recv_sem, ready_sem,
):
    ctx = lax.axis_index("ctx")
    chip, core = ctx // 2, lax.rem(ctx, 2)
    grp = lax.axis_index("grp")
    halves = (1 - grp, grp)

    def at(chip_to, core_to, grp_to):
        return {"ctx": chip_to * 2 + core_to, "grp": grp_to}

    def remote(src, dst, send, recv, to):
        return pltpu.make_async_remote_copy(
            src_ref=src, dst_ref=dst, send_sem=send, recv_sem=recv, device_id=to, device_id_type=MESH
        )

    def signal(sem, to):
        pl.semaphore_signal(sem, inc=1, device_id=to, device_id_type=MESH)

    twin = at(chip, 1 - core, grp)
    side = at(chip, core, 1 - grp)
    after = at(lax.rem(chip + 1, CHIPS), core, grp)

    loads = [
        pltpu.make_async_copy(src, dst, load_sem.at[i])
        for i, (src, dst) in enumerate((
            (k_hbm, kv.at[0]), (v_hbm, kv.at[1]),
            (q_hbm.at[:, columns(0)], q.at[pl.ds(0, BLOCK)]), (q_hbm.at[:, columns(1)], q.at[pl.ds(BLOCK, BLOCK)]),
            (g_hbm.at[:, columns(0)], g.at[pl.ds(0, BLOCK)]), (g_hbm.at[:, columns(1)], g.at[pl.ds(BLOCK, BLOCK)]),
        ))
    ]
    for copy in loads:
        copy.start()

    barrier = pltpu.get_barrier_semaphore()
    for step in range(1, CHIPS):
        @pl.when(chip + step < CHIPS)
        def _():
            for grp_to in (grp, 1 - grp):
                signal(barrier, at(chip + step, core, grp_to))
    signal(barrier, twin)
    signal(barrier, side)
    for copy in loads:
        copy.wait()
    pl.semaphore_wait(barrier, 2 + 2 * chip)

    @pl.when(chip == CHIPS - 1)
    def _():
        signal(ready_sem.at[1], at(0, core, grp))

    @pl.when(chip >= 1)
    def _():
        signal(ready_sem.at[0], at(chip - 1, core, grp))

    own, other = pl.ds(0, 2 * BLOCK), pl.ds(2 * BLOCK, 2 * BLOCK)
    swaps = (
        remote(q.at[own], q.at[other], other_send_sem.at[0], other_recv_sem.at[0], twin),
        remote(g.at[own], g.at[other], other_send_sem.at[1], other_recv_sem.at[1], twin),
    )
    for copy in swaps:
        copy.start()

    def kv_send(which, half):
        to, slot = ((after, 0), (at(CHIPS - 1, core, grp), 2))[which]
        return remote(
            kv.at[:, pl.ds(pl.multiple_of(half * HALF, HALF), HALF)], far_kv.at[slot, half],
            kv_send_sem.at[which, half], kv_recv_sem.at[slot, half], to,
        )

    def kv_pass(half):
        return remote(far_kv.at[0, half], far_kv.at[1, half], pass_send_sem.at[half], kv_recv_sem.at[1, half], after)

    def far_copy(step, half):
        slot = step - 1
        return remote(
            far_send.at[slot, half], far_recv.at[slot, grp], far_send_sem.at[slot, half],
            far_recv_sem.at[slot, grp], at(lax.rem(chip - step + CHIPS, CHIPS), core, half),
        )

    def near(rows, masked):
        scores = dot(kv[0], q[rows], (1, 1))
        mixing = dot(kv[1], g[rows], (1, 1))
        if masked:
            place = lax.broadcasted_iota(jnp.int32, (BLOCK, BLOCK), 0)
            seen_by = lax.broadcasted_iota(jnp.int32, (BLOCK, BLOCK), 1)
            seen = place <= seen_by
            scores = jnp.where(jnp.concatenate([seen, seen], 1), scores, 0.0)
        slopes[:, rows] = (scores * mixing).astype(BF16)
        low = (scores * scores).astype(BF16)
        return dot(slopes[:, rows], q[rows], (1, 0)), dot(low, g[rows], (1, 0))

    key_sum[...], value_sum[...] = near(own, True)

    @pl.when(chip < CHIPS - 1)
    def _():
        pl.semaphore_wait(ready_sem.at[0], 1)
        kv_send(0, halves[0]).start()

        @pl.when(chip < CHIPS - 2)
        def _():
            kv_send(0, halves[1]).start()

    for copy in swaps:
        copy.wait()

    @pl.when(core == 0)
    def _():
        key_part, value_part = near(other, False)
        key_sum[...] += key_part
        value_sum[...] += value_part

    @pl.when(core == 1)
    def _():
        slopes[:, other] = jnp.zeros((BLOCK, 2 * BLOCK), BF16)

    away = pl.ds(pl.multiple_of((1 - grp) * HALF, HALF), HALF)
    mine = pl.ds(pl.multiple_of(grp * HALF, HALF), HALF)
    side_send[:, columns(0)] = (key_sum[away] * SLOPE).astype(BF16)
    side_send[:, columns(1)] = (value_sum[away] * WEIGHT).astype(BF16)
    side_copy = remote(side_send, side_recv, side_send_sem, side_recv_sem, side)
    side_copy.start()

    @pl.when(chip == 0)
    def _():
        pl.semaphore_wait(ready_sem.at[1], 1)
        for half in halves:
            kv_send(1, half).start()

    query_sum[...] = dot(kv[0], slopes[...], (0, 0))

    def far(step, half, spare, passed=False):
        slot = step - 1
        remote(
            far_kv.at[slot, half], far_kv.at[slot, half], pass_send_sem.at[half], kv_recv_sem.at[slot, half], after
        ).wait_recv()
        if passed:
            kv_pass(half).start()
        scores = dot(far_kv[slot, half, 0], q[...], (1, 1))
        mixing = dot(far_kv[slot, half, 1], g[...], (1, 1))
        far_slopes[slot, half] = (scores * mixing).astype(BF16)
        weights[spare] = (scores * scores).astype(BF16)
        far_send[slot, half, :, columns(0)] = (dot(far_slopes[slot, half], q[...], (1, 0)) * SLOPE).astype(BF16)
        far_send[slot, half, :, columns(1)] = (dot(weights[spare], g[...], (1, 0)) * WEIGHT).astype(BF16)
        far_copy(step, half).start()

    def far_query(step):
        slot = step - 1
        for half in range(2):
            query_sum[...] += dot(far_kv[slot, half, 0], far_slopes[slot, half], (0, 0))

    @pl.when((chip >= 1) & (chip < CHIPS - 1))
    def _():
        far(1, halves[0], 0, True)
        far(1, halves[1], 1, True)

        @pl.when(chip == CHIPS - 2)
        def _():
            kv_send(0, halves[1]).start()
        far_query(1)

    @pl.when(chip == CHIPS - 2)
    def _():
        far(2, halves[0], 0)
        far(2, halves[1], 1)
        far_query(2)

    @pl.when(chip == CHIPS - 1)
    def _():
        for i, (step, half) in enumerate(((3, 0), (1, 0), (3, 1), (2, 0), (2, 1), (1, 1))):
            far(step, halves[half], i % 2)
        for step in (3, 2, 1):
            far_query(step)

    back = remote(query_sum.at[:, other], back_recv, back_send_sem, back_recv_sem, twin)
    back.start()
    back.wait()
    query_rows = ((query_sum[:, own] + back_recv[...]) * SLOPE).T
    for head in range(2):
        query_out[:, columns(head)] = query_rows[head * BLOCK:(head + 1) * BLOCK].astype(BF16)

    @pl.when(chip < CHIPS - 1)
    def _():
        for half in halves:
            kv_send(0, half).wait_send()

    @pl.when(chip == 0)
    def _():
        for half in halves:
            kv_send(1, half).wait_send()

    @pl.when((chip >= 1) & (chip < CHIPS - 1))
    def _():
        for half in halves:
            kv_pass(half).wait_send()

    side_copy.wait()
    key_sum[:HALF] = key_sum[mine] * SLOPE + side_recv[:, columns(0)].astype(F32)
    value_sum[:HALF] = value_sum[mine] * WEIGHT + side_recv[:, columns(1)].astype(F32)

    for step in range(1, CHIPS):
        slot = step - 1

        @pl.when(chip + step < CHIPS)
        def _():
            for grp_from in range(2):
                remote(
                    far_send.at[slot, 0], far_recv.at[slot, grp_from], far_send_sem.at[slot, 0],
                    far_recv_sem.at[slot, grp_from], side,
                ).wait_recv()
                key_sum[:HALF] += far_recv[slot, grp_from, :, columns(0)].astype(F32)
                value_sum[:HALF] += far_recv[slot, grp_from, :, columns(1)].astype(F32)

    for step in range(1, CHIPS):
        @pl.when(chip >= step)
        def _():
            for half in halves:
                far_copy(step, half).wait_send()
    key_out[...] = key_sum[:HALF].astype(BF16)
    value_out[...] = value_sum[:HALF].astype(BF16)


def finish(*refs):
    sem = refs[-1]
    copies = [pltpu.make_async_copy(refs[i], refs[3 + i], sem.at[i]) for i in range(3)]
    for copy in copies:
        copy.start()
    for copy in copies:
        copy.wait()


def local(queries, keys, values, out_grad):
    dma = pltpu.SemaphoreType.DMA
    done = pl.pallas_call(
        kernel,
        out_shape=(
            pltpu.VMEM((BLOCK, 2 * HEAD), BF16),
            pltpu.VMEM((HALF, HEAD), BF16),
            pltpu.VMEM((HALF, HEAD), BF16),
        ),
        in_specs=[pl.BlockSpec(memory_space=pl.ANY)] * 4,
        out_specs=(pl.BlockSpec(memory_space=pltpu.VMEM),) * 3,
        scratch_shapes=[
            pltpu.VMEM((4 * BLOCK, HEAD), BF16),
            pltpu.VMEM((4 * BLOCK, HEAD), BF16),
            pltpu.VMEM((2, BLOCK, HEAD), BF16),
            pltpu.VMEM((STEPS, 2, 2, HALF, HEAD), BF16),
            pltpu.VMEM((2, HALF, 4 * BLOCK), BF16),
            pltpu.VMEM((BLOCK, 4 * BLOCK), BF16),
            pltpu.VMEM((STEPS, 2, HALF, 4 * BLOCK), BF16),
            pltpu.VMEM((HEAD, 4 * BLOCK), F32),
            pltpu.VMEM((BLOCK, HEAD), F32),
            pltpu.VMEM((BLOCK, HEAD), F32),
            pltpu.VMEM((HEAD, 2 * BLOCK), F32),
            pltpu.VMEM((HALF, 2 * HEAD), BF16),
            pltpu.VMEM((HALF, 2 * HEAD), BF16),
            pltpu.VMEM((STEPS, 2, HALF, 2 * HEAD), BF16),
            pltpu.VMEM((STEPS, 2, HALF, 2 * HEAD), BF16),
            dma((6,)), dma((2,)), dma((2,)), dma((2, 2)), dma((2,)), dma((STEPS, 2)),
            dma((STEPS, 2)), dma((STEPS, 2)), dma, dma, dma, dma,
            pltpu.SemaphoreType.REGULAR((2,)),
        ],
        compiler_params=pltpu.CompilerParams(collective_id=0, has_side_effects=True),
    )(queries, keys, values, out_grad)
    return pl.pallas_call(
        finish,
        out_shape=tuple(jax.ShapeDtypeStruct(a.shape, a.dtype) for a in done),
        in_specs=[pl.BlockSpec(memory_space=pltpu.VMEM)] * 3,
        out_specs=(pl.BlockSpec(memory_space=pl.ANY),) * 3,
        scratch_shapes=[dma((3,))],
    )(*[pltpu.with_memory_space_constraint(a, pltpu.VMEM) for a in done])


def solution(mesh):
    return jax.shard_map(
        local,
        mesh=mesh,
        in_specs=(P("ctx", ("kv", "grp")), P("ctx", "kv"), P("ctx", "kv"), P("ctx", ("kv", "grp"))),
        out_specs=(P("ctx", ("kv", "grp")), P(("ctx", "grp"), "kv"), P(("ctx", "grp"), "kv")),
        check_vma=False,
    )
```

```python
import jax
import jax.numpy as jnp
from jax import lax
from jax.experimental import pallas as pl
from jax.experimental.pallas import tpu as pltpu
from jax.sharding import PartitionSpec as P

BLOCK = 256
HEAD = 128
HALF = 128
CHIPS = 4
STEPS = CHIPS - 1
MESH = pl.DeviceIdType.MESH
F32 = jnp.float32
BF16 = jnp.bfloat16
SLOPE = 2.0 / HEAD
WEIGHT = 1.0 / HEAD
RETURNS = (1, 3, 2)
ORDERS = ((), ((1, 0), None, (1, 1)), ((1, 0), (1, 1), None, (2, 0), (2, 1)), ((3, 0), (1, 0), (3, 1), (2, 0), (2, 1), (1, 1)))


def dot(a, b, contract):
    return lax.dot_general(a, b, ((contract[:1], contract[1:]), ((), ())), preferred_element_type=F32)


def columns(head):
    return slice(head * HEAD, (head + 1) * HEAD)


def kernel(
    q_hbm, k_hbm, v_hbm, g_hbm,
    query_out, key_out, value_out,
    q, g, kv, far_kv, weights, slopes, far_slopes,
    query_sum, key_sum, value_sum, back_recv, side_send, side_recv, far_send, far_recv,
    load_sem, swap_send_sem, swap_recv_sem, kv_send_sem, wrap_send_sem, pass_send_sem, kv_recv_sem,
    far_send_sem, far_recv_sem, side_send_sem, side_recv_sem, back_send_sem, back_recv_sem,
    ready_sem,
):
    ctx = lax.axis_index("ctx")
    chip, core = ctx // 2, lax.rem(ctx, 2)
    grp = lax.axis_index("grp")
    halves = (1 - grp, grp)
    first, last = chip == 0, chip == CHIPS - 1
    inner = (chip >= 1) & (chip < CHIPS - 1)

    def at(chip_to, core_to, grp_to):
        return {"ctx": chip_to * 2 + core_to, "grp": grp_to}

    def remote(src, dst, send, recv, to):
        return pltpu.make_async_remote_copy(
            src_ref=src, dst_ref=dst, send_sem=send, recv_sem=recv, device_id=to, device_id_type=MESH
        )

    def signal(sem, to):
        pl.semaphore_signal(sem, inc=1, device_id=to, device_id_type=MESH)

    twin, side = at(chip, 1 - core, grp), at(chip, core, 1 - grp)
    after = at(lax.rem(chip + 1, CHIPS), core, grp)
    wrap = at(CHIPS - 1, core, grp)

    loads = [
        pltpu.make_async_copy(src, dst, load_sem.at[i])
        for i, (src, dst) in enumerate((
            (k_hbm, kv.at[0]), (v_hbm, kv.at[1]),
            (q_hbm.at[:, columns(0)], q.at[pl.ds(0, BLOCK)]), (q_hbm.at[:, columns(1)], q.at[pl.ds(BLOCK, BLOCK)]),
            (g_hbm.at[:, columns(0)], g.at[pl.ds(0, BLOCK)]), (g_hbm.at[:, columns(1)], g.at[pl.ds(BLOCK, BLOCK)]),
        ))
    ]
    for copy in loads:
        copy.start()

    barrier = pltpu.get_barrier_semaphore()

    @pl.when(chip >= 1)
    def _():
        signal(barrier, at(chip - 1, core, grp))

    @pl.when(chip < CHIPS - 1)
    def _():
        signal(barrier, at(chip + 1, core, grp))

    @pl.when(first)
    def _():
        signal(barrier, wrap)
    signal(barrier, side)
    signal(barrier, twin)
    pl.semaphore_wait(barrier, jnp.where(first, 3, 4))

    @pl.when(last)
    def _():
        signal(ready_sem, at(0, core, grp))

    own, other = pl.ds(0, 2 * BLOCK), pl.ds(2 * BLOCK, 2 * BLOCK)
    swaps = (
        remote(q.at[own], q.at[other], swap_send_sem.at[0], swap_recv_sem.at[0], twin),
        remote(g.at[own], g.at[other], swap_send_sem.at[1], swap_recv_sem.at[1], twin),
    )
    side_copy = remote(side_send, side_recv, side_send_sem, side_recv_sem, side)

    def kv_rows(half):
        return kv.at[:, pl.ds(pl.multiple_of(half * HALF, HALF), HALF)]

    def kv_send(half):
        return remote(kv_rows(half), far_kv.at[0, half], kv_send_sem.at[half], kv_recv_sem.at[0, half], after)

    def kv_wrap(half):
        return remote(kv_rows(half), far_kv.at[2, half], wrap_send_sem.at[half], kv_recv_sem.at[2, half], wrap)

    def kv_pass(half):
        return remote(far_kv.at[0, half], far_kv.at[1, half], pass_send_sem.at[half], kv_recv_sem.at[1, half], after)

    def far_copy(step, half):
        slot = step - 1
        return remote(
            far_send.at[slot, half], far_recv.at[slot, grp], far_send_sem.at[slot, half],
            far_recv_sem.at[slot, grp], at(lax.rem(chip + CHIPS - step, CHIPS), core, half),
        )

    def near(rows, masked):
        scores = dot(kv[0], q[rows], (1, 1))
        mixing = dot(kv[1], g[rows], (1, 1))
        if masked:
            place = lax.broadcasted_iota(jnp.int32, (BLOCK, BLOCK), 0)
            seen_by = lax.broadcasted_iota(jnp.int32, (BLOCK, BLOCK), 1)
            seen = place <= seen_by
            scores = jnp.where(jnp.concatenate([seen, seen], 1), scores, 0.0)
        slopes[:, rows] = (scores * mixing).astype(BF16)
        low = (scores * scores).astype(BF16)
        return dot(slopes[:, rows], q[rows], (1, 0)), dot(low, g[rows], (1, 0))

    away = pl.ds(pl.multiple_of((1 - grp) * HALF, HALF), HALF)
    mine = pl.ds(pl.multiple_of(grp * HALF, HALF), HALF)

    def near_rest():
        @pl.when(core == 0)
        def _():
            key_part, value_part = near(other, False)
            key_sum[...] += key_part
            value_sum[...] += value_part

        @pl.when(core == 1)
        def _():
            slopes[:, other] = jnp.zeros((BLOCK, 2 * BLOCK), BF16)

        side_send[:, columns(0)] = (key_sum[away] * SLOPE).astype(BF16)
        side_send[:, columns(1)] = (value_sum[away] * WEIGHT).astype(BF16)
        side_copy.start()

    def far(step, half, spare, passing):
        slot = step - 1
        kv_arrival(slot, half).wait_recv()
        if passing:
            kv_pass(half).start()
        scores = dot(far_kv[slot, half, 0], q[...], (1, 1))
        mixing = dot(far_kv[slot, half, 1], g[...], (1, 1))
        far_slopes[slot, half] = (scores * mixing).astype(BF16)
        weights[spare] = (scores * scores).astype(BF16)
        far_send[slot, half, :, columns(0)] = (dot(far_slopes[slot, half], q[...], (1, 0)) * SLOPE).astype(BF16)
        far_send[slot, half, :, columns(1)] = (dot(weights[spare], g[...], (1, 0)) * WEIGHT).astype(BF16)
        far_copy(step, half).start()

    def kv_arrival(slot, half):
        return remote(
            far_kv.at[slot, half], far_kv.at[slot, half], pass_send_sem.at[half], kv_recv_sem.at[slot, half], after
        )

    def far_query(step):
        slot = step - 1
        for half in range(2):
            query_sum[...] += dot(far_kv[slot, half, 0], far_slopes[slot, half], (0, 0))

    for copy in loads:
        copy.wait()

    @pl.when(chip < CHIPS - 1)
    def _():
        kv_send(halves[0]).start()

    @pl.when(first)
    def _():
        kv_send(halves[1]).start()
    for copy in swaps:
        copy.start()
    key_sum[...], value_sum[...] = near(own, True)
    for copy in swaps:
        copy.wait()

    @pl.when(first)
    def _():
        near_rest()
        pl.semaphore_wait(ready_sem, 1)
        for half in halves:
            kv_wrap(half).start()
        query_sum[...] = dot(kv[0], slopes[...], (0, 0))

    for chip_at, order in enumerate(ORDERS):
        @pl.when(chip == chip_at)
        def _():
            for i, what in enumerate(order):
                if what is None:
                    kv_send(halves[1]).start()
                else:
                    far(what[0], halves[what[1]], i % 2, what[0] == 1 and chip_at < CHIPS - 1)

    @pl.when(chip >= 1)
    def _():
        near_rest()
        query_sum[...] = dot(kv[0], slopes[...], (0, 0))
        far_query(1)

        @pl.when(chip >= 2)
        def _():
            far_query(2)

        @pl.when(last)
        def _():
            far_query(3)

    back = remote(query_sum.at[:, other], back_recv, back_send_sem, back_recv_sem, twin)
    back.start()

    back.wait()
    query_rows = ((query_sum[:, own] + back_recv[...]) * SLOPE).T
    for head in range(2):
        query_out[:, columns(head)] = query_rows[head * BLOCK:(head + 1) * BLOCK].astype(BF16)

    side_copy.wait()
    key_sum[:HALF] = key_sum[mine] * SLOPE + side_recv[:, columns(0)].astype(F32)
    value_sum[:HALF] = value_sum[mine] * WEIGHT + side_recv[:, columns(1)].astype(F32)

    @pl.when(chip < CHIPS - 1)
    def _():
        for half in halves:
            kv_send(half).wait_send()

    @pl.when(first)
    def _():
        for half in halves:
            kv_wrap(half).wait_send()

    @pl.when(inner)
    def _():
        for half in halves:
            kv_pass(half).wait_send()

    for step in RETURNS:
        slot = step - 1

        @pl.when(chip + step < CHIPS)
        def _():
            for grp_from in range(2):
                far_in = remote(
                    far_send.at[slot, 0], far_recv.at[slot, grp_from], far_send_sem.at[slot, 0],
                    far_recv_sem.at[slot, grp_from], after,
                )
                far_in.wait_recv()
                key_sum[:HALF] += far_recv[slot, grp_from, :, columns(0)].astype(F32)
                value_sum[:HALF] += far_recv[slot, grp_from, :, columns(1)].astype(F32)

    for step in range(1, CHIPS):
        @pl.when(chip >= step)
        def _():
            for half in halves:
                far_copy(step, half).wait_send()
    key_out[...] = key_sum[:HALF].astype(BF16)
    value_out[...] = value_sum[:HALF].astype(BF16)


def finish(*refs):
    sem = refs[-1]
    copies = [pltpu.make_async_copy(refs[i], refs[3 + i], sem.at[i]) for i in range(3)]
    for copy in copies:
        copy.start()
    for copy in copies:
        copy.wait()


def local(queries, keys, values, out_grad):
    dma = pltpu.SemaphoreType.DMA
    done = pl.pallas_call(
        kernel,
        out_shape=(
            pltpu.VMEM((BLOCK, 2 * HEAD), BF16),
            pltpu.VMEM((HALF, HEAD), BF16),
            pltpu.VMEM((HALF, HEAD), BF16),
        ),
        in_specs=[pl.BlockSpec(memory_space=pl.ANY)] * 4,
        out_specs=(pl.BlockSpec(memory_space=pltpu.VMEM),) * 3,
        scratch_shapes=[
            pltpu.VMEM((4 * BLOCK, HEAD), BF16),
            pltpu.VMEM((4 * BLOCK, HEAD), BF16),
            pltpu.VMEM((2, BLOCK, HEAD), BF16),
            pltpu.VMEM((STEPS, 2, 2, HALF, HEAD), BF16),
            pltpu.VMEM((2, HALF, 4 * BLOCK), BF16),
            pltpu.VMEM((BLOCK, 4 * BLOCK), BF16),
            pltpu.VMEM((STEPS, 2, HALF, 4 * BLOCK), BF16),
            pltpu.VMEM((HEAD, 4 * BLOCK), F32),
            pltpu.VMEM((BLOCK, HEAD), F32),
            pltpu.VMEM((BLOCK, HEAD), F32),
            pltpu.VMEM((HEAD, 2 * BLOCK), F32),
            pltpu.VMEM((HALF, 2 * HEAD), BF16),
            pltpu.VMEM((HALF, 2 * HEAD), BF16),
            pltpu.VMEM((STEPS, 2, HALF, 2 * HEAD), BF16),
            pltpu.VMEM((STEPS, 2, HALF, 2 * HEAD), BF16),
            dma((6,)), dma((2,)), dma((2,)), dma((2,)), dma((2,)), dma((2,)), dma((STEPS, 2)),
            dma((STEPS, 2)), dma((STEPS, 2)), dma, dma, dma, dma,
            pltpu.SemaphoreType.REGULAR,
        ],
        compiler_params=pltpu.CompilerParams(collective_id=0, has_side_effects=True),
    )(queries, keys, values, out_grad)
    return pl.pallas_call(
        finish,
        out_shape=tuple(jax.ShapeDtypeStruct(a.shape, a.dtype) for a in done),
        in_specs=[pl.BlockSpec(memory_space=pltpu.VMEM)] * 3,
        out_specs=(pl.BlockSpec(memory_space=pl.ANY),) * 3,
        scratch_shapes=[dma((3,))],
    )(*[pltpu.with_memory_space_constraint(a, pltpu.VMEM) for a in done])


def solution(mesh):
    return jax.shard_map(
        local,
        mesh=mesh,
        in_specs=(P("ctx", ("kv", "grp")), P("ctx", "kv"), P("ctx", "kv"), P("ctx", ("kv", "grp"))),
        out_specs=(P("ctx", ("kv", "grp")), P(("ctx", "grp"), "kv"), P(("ctx", "grp"), "kv")),
        check_vma=False,
    )
```

```python
import jax
import jax.numpy as jnp
from jax import lax
from jax.experimental import pallas as pl
from jax.experimental.pallas import tpu as pltpu
from jax.sharding import PartitionSpec as P

BLOCK = 256
HEAD = 128
HALF = 128
CHIPS = 4
STEPS = CHIPS - 1
MESH = pl.DeviceIdType.MESH
F32 = jnp.float32
BF16 = jnp.bfloat16
SLOPE = 2.0 / HEAD
WEIGHT = 1.0 / HEAD
ORDERS = ((), ((1, 0), None, (1, 1)), ((1, 0), (1, 1), None, (2, 0), (2, 1)), ((3, 0), (1, 0), (3, 1), (2, 0), (2, 1), (1, 1)))


def dot(a, b, contract):
    return lax.dot_general(a, b, ((contract[:1], contract[1:]), ((), ())), preferred_element_type=F32)


def columns(head):
    return slice(head * HEAD, (head + 1) * HEAD)


def kernel(
    q_hbm, k_hbm, v_hbm, g_hbm,
    query_out, key_out, value_out,
    q, g, kv, far_kv, weights, slopes, far_slopes,
    query_sum, key_sum, value_sum, back_recv, side_send, side_recv, far_send, far_recv,
    load_sem, swap_send_sem, swap_recv_sem, kv_send_sem, wrap_send_sem, pass_send_sem, kv_recv_sem,
    far_send_sem, far_recv_sem, side_send_sem, side_recv_sem, back_send_sem, back_recv_sem,
    ready_sem,
):
    ctx = lax.axis_index("ctx")
    chip, core = ctx // 2, lax.rem(ctx, 2)
    grp = lax.axis_index("grp")
    halves = (1 - grp, grp)
    first, last = chip == 0, chip == CHIPS - 1
    inner = (chip >= 1) & (chip < CHIPS - 1)

    def at(chip_to, core_to, grp_to):
        return {"ctx": chip_to * 2 + core_to, "grp": grp_to}

    def remote(src, dst, send, recv, to):
        return pltpu.make_async_remote_copy(
            src_ref=src, dst_ref=dst, send_sem=send, recv_sem=recv, device_id=to, device_id_type=MESH
        )

    def signal(sem, to):
        pl.semaphore_signal(sem, inc=1, device_id=to, device_id_type=MESH)

    twin, side = at(chip, 1 - core, grp), at(chip, core, 1 - grp)
    after = at(lax.rem(chip + 1, CHIPS), core, grp)
    wrap = at(CHIPS - 1, core, grp)

    loads = [
        pltpu.make_async_copy(src, dst, load_sem.at[i])
        for i, (src, dst) in enumerate((
            (k_hbm, kv.at[0]), (v_hbm, kv.at[1]),
            (q_hbm.at[:, columns(0)], q.at[pl.ds(0, BLOCK)]), (q_hbm.at[:, columns(1)], q.at[pl.ds(BLOCK, BLOCK)]),
            (g_hbm.at[:, columns(0)], g.at[pl.ds(0, BLOCK)]), (g_hbm.at[:, columns(1)], g.at[pl.ds(BLOCK, BLOCK)]),
        ))
    ]
    for copy in loads:
        copy.start()

    barrier = pltpu.get_barrier_semaphore()

    @pl.when(chip >= 1)
    def _():
        signal(barrier, at(chip - 1, core, grp))

    @pl.when(chip < CHIPS - 1)
    def _():
        signal(barrier, at(chip + 1, core, grp))

    @pl.when(first)
    def _():
        signal(barrier, wrap)
    signal(barrier, side)
    signal(barrier, twin)
    pl.semaphore_wait(barrier, jnp.where(first, 3, 4))

    @pl.when(last)
    def _():
        signal(ready_sem, at(0, core, grp))

    own, other = pl.ds(0, 2 * BLOCK), pl.ds(2 * BLOCK, 2 * BLOCK)
    swaps = (
        remote(q.at[own], q.at[other], swap_send_sem.at[0], swap_recv_sem.at[0], twin),
        remote(g.at[own], g.at[other], swap_send_sem.at[1], swap_recv_sem.at[1], twin),
    )
    side_copy = remote(side_send, side_recv, side_send_sem, side_recv_sem, side)

    def kv_rows(half):
        return kv.at[:, pl.ds(pl.multiple_of(half * HALF, HALF), HALF)]

    def kv_send(half):
        return remote(kv_rows(half), far_kv.at[0, half], kv_send_sem.at[half], kv_recv_sem.at[0, half], after)

    def kv_wrap(half):
        return remote(kv_rows(half), far_kv.at[2, half], wrap_send_sem.at[half], kv_recv_sem.at[2, half], wrap)

    def kv_pass(half):
        return remote(far_kv.at[0, half], far_kv.at[1, half], pass_send_sem.at[half], kv_recv_sem.at[1, half], after)

    def far_copy(step, half):
        slot = step - 1
        return remote(
            far_send.at[slot, half], far_recv.at[slot, grp], far_send_sem.at[slot, half],
            far_recv_sem.at[slot, grp], at(lax.rem(chip + CHIPS - step, CHIPS), core, half),
        )

    def near(rows, masked):
        scores = dot(kv[0], q[rows], (1, 1))
        mixing = dot(kv[1], g[rows], (1, 1))
        if masked:
            place = lax.broadcasted_iota(jnp.int32, (BLOCK, BLOCK), 0)
            seen_by = lax.broadcasted_iota(jnp.int32, (BLOCK, BLOCK), 1)
            seen = place <= seen_by
            scores = jnp.where(jnp.concatenate([seen, seen], 1), scores, 0.0)
        slopes[:, rows] = (scores * mixing).astype(BF16)
        low = (scores * scores).astype(BF16)
        return dot(slopes[:, rows], q[rows], (1, 0)), dot(low, g[rows], (1, 0))

    away = pl.ds(pl.multiple_of((1 - grp) * HALF, HALF), HALF)
    mine = pl.ds(pl.multiple_of(grp * HALF, HALF), HALF)

    def near_rest():
        @pl.when(core == 0)
        def _():
            key_part, value_part = near(other, False)
            key_sum[...] += key_part
            value_sum[...] += value_part

        @pl.when(core == 1)
        def _():
            slopes[:, other] = jnp.zeros((BLOCK, 2 * BLOCK), BF16)

        side_send[:, columns(0)] = (key_sum[away] * SLOPE).astype(BF16)
        side_send[:, columns(1)] = (value_sum[away] * WEIGHT).astype(BF16)
        side_copy.start()

    def far(step, half, spare, passing):
        slot = step - 1
        kv_arrival(slot, half).wait_recv()
        if passing:
            kv_pass(half).start()
        scores = dot(far_kv[slot, half, 0], q[...], (1, 1))
        mixing = dot(far_kv[slot, half, 1], g[...], (1, 1))
        far_slopes[slot, half] = (scores * mixing).astype(BF16)
        weights[spare] = (scores * scores).astype(BF16)
        far_send[slot, half, :, columns(0)] = (dot(far_slopes[slot, half], q[...], (1, 0)) * SLOPE).astype(BF16)
        far_send[slot, half, :, columns(1)] = (dot(weights[spare], g[...], (1, 0)) * WEIGHT).astype(BF16)
        far_copy(step, half).start()

    def kv_arrival(slot, half):
        return remote(
            far_kv.at[slot, half], far_kv.at[slot, half], pass_send_sem.at[half], kv_recv_sem.at[slot, half], after
        )

    def far_query(step):
        slot = step - 1
        for half in range(2):
            query_sum[...] += dot(far_kv[slot, half, 0], far_slopes[slot, half], (0, 0))

    for copy in loads:
        copy.wait()

    @pl.when(chip < CHIPS - 1)
    def _():
        kv_send(halves[0]).start()

    @pl.when(first)
    def _():
        kv_send(halves[1]).start()
    for copy in swaps:
        copy.start()
    key_sum[...], value_sum[...] = near(own, True)
    for copy in swaps:
        copy.wait()

    @pl.when(first)
    def _():
        near_rest()
        pl.semaphore_wait(ready_sem, 1)
        for half in halves:
            kv_wrap(half).start()
        query_sum[...] = dot(kv[0], slopes[...], (0, 0))

    for chip_at, order in enumerate(ORDERS):
        @pl.when(chip == chip_at)
        def _():
            for i, what in enumerate(order):
                if what is None:
                    kv_send(halves[1]).start()
                else:
                    far(what[0], halves[what[1]], i % 2, what[0] == 1 and chip_at < CHIPS - 1)

    @pl.when(chip >= 1)
    def _():
        near_rest()
        query_sum[...] = dot(kv[0], slopes[...], (0, 0))
        far_query(1)

        @pl.when(chip >= 2)
        def _():
            far_query(2)

        @pl.when(last)
        def _():
            far_query(3)

    back = remote(query_sum.at[:, other], back_recv, back_send_sem, back_recv_sem, twin)
    back.start()

    back.wait()
    query_rows = ((query_sum[:, own] + back_recv[...]) * SLOPE).T
    for head in range(2):
        query_out[:, columns(head)] = query_rows[head * BLOCK:(head + 1) * BLOCK].astype(BF16)

    side_copy.wait()
    key_sum[:HALF] = key_sum[mine] * SLOPE + side_recv[:, columns(0)].astype(F32)
    value_sum[:HALF] = value_sum[mine] * WEIGHT + side_recv[:, columns(1)].astype(F32)

    @pl.when(chip < CHIPS - 1)
    def _():
        for half in halves:
            kv_send(half).wait_send()

    @pl.when(first)
    def _():
        for half in halves:
            kv_wrap(half).wait_send()

    @pl.when(inner)
    def _():
        for half in halves:
            kv_pass(half).wait_send()

    def returned(step):
        slot = step - 1
        for grp_from in range(2):
            far_in = remote(
                far_send.at[slot, 0], far_recv.at[slot, grp_from], far_send_sem.at[slot, 0],
                far_recv_sem.at[slot, grp_from], side,
            )
            far_in.wait_recv()
        both = far_recv[slot, 0].astype(F32) + far_recv[slot, 1].astype(F32)
        return key_sum[:HALF] + both[:, columns(0)], value_sum[:HALF] + both[:, columns(1)]

    def give(key_total, value_total):
        key_out[...] = key_total.astype(BF16)
        value_out[...] = value_total.astype(BF16)

    for step in range(2, CHIPS):
        @pl.when(chip >= step)
        def _():
            for half in halves:
                far_copy(step, half).wait_send()

    for step in (1, 3):
        @pl.when(chip + step < CHIPS)
        def _():
            key_sum[:HALF], value_sum[:HALF] = returned(step)

    @pl.when(chip >= 1)
    def _():
        for half in halves:
            far_copy(1, half).wait_send()

    @pl.when(chip < CHIPS - 2)
    def _():
        give(*returned(2))

    @pl.when(chip >= CHIPS - 2)
    def _():
        give(key_sum[:HALF], value_sum[:HALF])


def finish(*refs):
    sem = refs[-1]
    copies = [pltpu.make_async_copy(refs[i], refs[3 + i], sem.at[i]) for i in range(3)]
    for copy in copies:
        copy.start()
    for copy in copies:
        copy.wait()


def local(queries, keys, values, out_grad):
    dma = pltpu.SemaphoreType.DMA
    done = pl.pallas_call(
        kernel,
        out_shape=(
            pltpu.VMEM((BLOCK, 2 * HEAD), BF16),
            pltpu.VMEM((HALF, HEAD), BF16),
            pltpu.VMEM((HALF, HEAD), BF16),
        ),
        in_specs=[pl.BlockSpec(memory_space=pl.ANY)] * 4,
        out_specs=(pl.BlockSpec(memory_space=pltpu.VMEM),) * 3,
        scratch_shapes=[
            pltpu.VMEM((4 * BLOCK, HEAD), BF16),
            pltpu.VMEM((4 * BLOCK, HEAD), BF16),
            pltpu.VMEM((2, BLOCK, HEAD), BF16),
            pltpu.VMEM((STEPS, 2, 2, HALF, HEAD), BF16),
            pltpu.VMEM((2, HALF, 4 * BLOCK), BF16),
            pltpu.VMEM((BLOCK, 4 * BLOCK), BF16),
            pltpu.VMEM((STEPS, 2, HALF, 4 * BLOCK), BF16),
            pltpu.VMEM((HEAD, 4 * BLOCK), F32),
            pltpu.VMEM((BLOCK, HEAD), F32),
            pltpu.VMEM((BLOCK, HEAD), F32),
            pltpu.VMEM((HEAD, 2 * BLOCK), F32),
            pltpu.VMEM((HALF, 2 * HEAD), BF16),
            pltpu.VMEM((HALF, 2 * HEAD), BF16),
            pltpu.VMEM((STEPS, 2, HALF, 2 * HEAD), BF16),
            pltpu.VMEM((STEPS, 2, HALF, 2 * HEAD), BF16),
            dma((6,)), dma((2,)), dma((2,)), dma((2,)), dma((2,)), dma((2,)), dma((STEPS, 2)),
            dma((STEPS, 2)), dma((STEPS, 2)), dma, dma, dma, dma,
            pltpu.SemaphoreType.REGULAR,
        ],
        compiler_params=pltpu.CompilerParams(collective_id=0, has_side_effects=True),
    )(queries, keys, values, out_grad)
    return pl.pallas_call(
        finish,
        out_shape=tuple(jax.ShapeDtypeStruct(a.shape, a.dtype) for a in done),
        in_specs=[pl.BlockSpec(memory_space=pltpu.VMEM)] * 3,
        out_specs=(pl.BlockSpec(memory_space=pl.ANY),) * 3,
        scratch_shapes=[dma((3,))],
    )(*[pltpu.with_memory_space_constraint(a, pltpu.VMEM) for a in done])


def solution(mesh):
    return jax.shard_map(
        local,
        mesh=mesh,
        in_specs=(P("ctx", ("kv", "grp")), P("ctx", "kv"), P("ctx", "kv"), P("ctx", ("kv", "grp"))),
        out_specs=(P("ctx", ("kv", "grp")), P(("ctx", "grp"), "kv"), P(("ctx", "grp"), "kv")),
        check_vma=False,
    )
```
